128 devices in a mesh: row: 16 (over y, x), col: 8 (over z, core).
Axes of the slice: x: 4, y: 4, z: 4, core: 2. Of those that a mesh axis runs over, the one named last changes fastest.
Arguments:
- activations: bfloat16 [1024, 32, 8192], P(('row', 'col')), may hold values from -6 to 6
- out_grads: bfloat16 [1024, 32, 8192], P(('row', 'col')), may hold values from -6 to 6
- proj_in: bfloat16 [8192, 64], replicated, may hold values from -0.0625 to 0.0625
- proj_out: bfloat16 [8192, 64], replicated, may hold values from -0.0625 to 0.0625
- damp_level: int32 [4096], replicated, may hold values from 1 to 4
Outputs:
- factored: float32 [4096, 4096], P('row', 'col')
The draws below stay inside these ranges and needn't reach their ends.
All inputs are finite; a program needn't handle non-finite values.
Results may differ from the reference program's by a relative error of at most 0.0033.
Values may be sent and summed in bfloat16 or wider, within the bound.
A program may use at most 64 MiB of HBM per device.

```python
import jax
import jax.numpy as jnp
from jax import lax

D = 8192
R = 64
PANEL = 128
TOK_EX = 32
K = 4096
EXAMPLES = 1024


def place_ends(entries, key, smallest, top_value):
    longest = entries.shape.index(max(entries.shape))
    spots = []
    for shift in (0, 1):
        where = [jax.random.randint(jax.random.fold_in(key, axis), (), 0, length) for axis, length in enumerate(entries.shape)]
        where[longest] = (where[longest] + shift) % entries.shape[longest]
        spots.append(tuple(where))
    return entries.at[spots[0]].set(smallest).at[spots[1]].set(top_value)


def block_scale(key, shape, cuts, smallest, top_value):
    level = 1.0
    for axis_at, blocks in cuts:
        draws = jax.random.uniform(jax.random.fold_in(jax.random.fold_in(key, 6), axis_at), (blocks,), jnp.float32, smallest / len(cuts), top_value / len(cuts))
        level = level * jnp.repeat(jnp.exp(draws), shape[axis_at] // blocks).reshape((-1,) + (1,) * (len(shape) - 1 - axis_at))
    return level


def normal_values(rng, shape, deviation, limit, shards=(), kind=jnp.bfloat16):
    loudness = block_scale(rng, shape, shards, -0.22, 0.18) if shards else 1.0
    drawn = jax.random.normal(rng, shape, jnp.float32) * deviation * loudness
    return jnp.minimum(jnp.maximum(drawn, -limit), limit).astype(kind)


def setup_inputs(seed: int = 0) -> dict:
    splits = jax.random.split(jax.random.key(seed), 6)
    return {
        "activations": normal_values(splits[0], (EXAMPLES, TOK_EX, D), 1.0, 6.0, ((0, 128),)),
        "out_grads": normal_values(splits[1], (EXAMPLES, TOK_EX, D), 1.0, 6.0, ((0, 128),)),
        "proj_in": normal_values(splits[2], (D, R), D ** -0.5, 0.0625),
        "proj_out": normal_values(splits[3], (D, R), D ** -0.5, 0.0625),
        "damp_level": place_ends(jax.random.randint(splits[4], (K,), 1, 5), jax.random.fold_in(splits[4], 1), 1, 4).astype(jnp.int32),
    }


damp_coef = 0.25

def project_one(pair):
    act_one, grad_one, proj_a, proj_g = pair
    a_proj = jnp.dot(act_one.astype(jnp.float32), proj_a.astype(jnp.float32), precision=lax.Precision.HIGHEST)
    g_proj = jnp.dot(grad_one.astype(jnp.float32), proj_g.astype(jnp.float32), precision=lax.Precision.HIGHEST)
    outer = jnp.dot(g_proj.T, a_proj, precision=lax.Precision.HIGHEST) * TOK_EX ** (-0.5)
    return outer.reshape(-1).astype(jnp.bfloat16)

def reference(activations, out_grads, proj_in, proj_out, damp_level):
    grads = lax.map(lambda item: project_one((item[0], item[1], proj_in, proj_out)), (activations, out_grads))
    wide = grads.astype(jnp.float32)
    total_sq = jnp.sum(wide * wide)
    damping = damp_coef * total_sq / (EXAMPLES * K)
    fisher = jnp.dot(wide.T, wide, precision=lax.Precision.HIGHEST) / EXAMPLES
    diag_index = jnp.arange(K)
    fisher = fisher.at[diag_index, diag_index].add(damping * damp_level.astype(jnp.float32))
    for panel_no in range(2):
        first = panel_no * PANEL
        beyond = first + PANEL
        lower = jnp.linalg.cholesky(fisher[first:beyond, first:beyond])
        left_panel = jax.scipy.linalg.solve_triangular(lower, fisher[beyond:, first:beyond].T, lower=True).T
        update = jnp.dot(left_panel, left_panel.T, precision=lax.Precision.HIGHEST)
        fisher = fisher.at[beyond:, beyond:].add(-update)
        fisher = fisher.at[first:beyond, first:beyond].set(jnp.tril(lower))
        fisher = fisher.at[beyond:, first:beyond].set(left_panel)
        fisher = fisher.at[first:beyond, beyond:].set(jnp.zeros((PANEL, K - beyond), jnp.float32))
    return fisher
```

```python
import functools

import jax
import jax.numpy as jnp
from jax import lax
from jax.experimental import pallas as pl
from jax.experimental.pallas import tpu as pltpu
from jax.sharding import PartitionSpec as P

F32, BF16 = jnp.float32, jnp.bfloat16
MESH = pl.DeviceIdType.MESH
HIGHEST = lax.Precision.HIGHEST
PANEL = 128
damp_coef = 0.25
CHUNKS = 8


def nn(a, b, precision=None):
    return lax.dot_general(a, b, (((1,), (0,)), ((), ())), precision=precision, preferred_element_type=F32)


def nt(a, b, precision=None):
    return lax.dot_general(a, b, (((1,), (1,)), ((), ())), precision=precision, preferred_element_type=F32)


def inv_chol(m3, emit):
    lane = lax.broadcasted_iota(jnp.int32, (8, 128), 1)
    for k in range(16):
        for o in (0, 4):
            j = 8 * k + o
            inside = (lane >= j) & (lane < j + 4)
            cols = [jnp.broadcast_to(m3[:, :, j + a : j + a + 1], m3.shape) for a in range(4)]

            def splat(b, a):
                return jnp.broadcast_to(cols[a][0, o + b : o + b + 1, :], (8, 128))

            def row(b):
                wide = jnp.broadcast_to(m3[0, o + b : o + b + 1, :], (8, 128))
                return jnp.where(inside, jnp.where(lane == j + b, 1.0, 0.0), wide)

            p00, p10, p11 = splat(0, 0), splat(1, 0), splat(1, 1)
            q00, q01, q10, q11 = splat(2, 0), splat(2, 1), splat(3, 0), splat(3, 1)
            p22, p32, p33 = splat(2, 2), splat(3, 2), splat(3, 3)
            r0, r1, r2, r3 = (row(b) for b in range(4))
            d1 = 1.0 / (p00 * p11 - p10 * p10)
            i00, i01, i11 = p11 * d1, -p10 * d1, p00 * d1
            t00, t01 = q00 * i00 + q01 * i01, q00 * i01 + q01 * i11
            t10, t11 = q10 * i00 + q11 * i01, q10 * i01 + q11 * i11
            s00 = p22 - (t00 * q00 + t01 * q01)
            s10 = p32 - (t10 * q00 + t11 * q01)
            s11 = p33 - (t10 * q10 + t11 * q11)
            d2 = 1.0 / (s00 * s11 - s10 * s10)
            y2 = r2 - (t00 * r0 + t01 * r1)
            y3 = r3 - (t10 * r0 + t11 * r1)
            e00, e01, e11 = s11 * d2, -s10 * d2, s00 * d2
            w2 = e00 * y2 + e01 * y3
            w3 = e01 * y2 + e11 * y3
            w0 = (i00 * r0 + i01 * r1) - (t00 * w2 + t10 * w3)
            w1 = (i01 * r0 + i11 * r1) - (t01 * w2 + t11 * w3)
            u0 = lax.rsqrt(p00)
            f1 = p10 * (u0 * u0)
            g1 = lax.rsqrt(p11 - f1 * p10)
            u2 = lax.rsqrt(s00)
            f3 = s10 * (u2 * u2)
            g3 = lax.rsqrt(s11 - f3 * s10)
            keep = lane < j + 4
            rows = (r0 * u0, (r1 - f1 * r0) * g1, y2 * u2, (y3 - f3 * y2) * g3)
            for b in range(4):
                emit(j + b, jnp.where(keep, rows[b], 0.0)[0:1, :])
            if j + 4 < PANEL:
                base = jnp.where(inside[None], 0.0, m3)
                m3 = base - (cols[0] * w0[None] + cols[1] * w1[None] + cols[2] * w2[None] + cols[3] * w3[None])
        if k < 15:
            m3 = m3[1:]


def body(
    n_rows, n_cols, act, outg, pin, pout, damp, out,
    xa, xg, wa, wg, own, pa, ca, ra, own_sq, pb, sq, cb, rb, amat, inv1, inv2,
    in_sem, pa_s, pa_r, ca_s, ca_r, ra_s, ra_r, pb_s, pb_r, sq_s, sq_r, cb_s, cb_r, rb_s, rb_r,
):
    r, c = lax.axis_index("row"), lax.axis_index("col")
    total_ex = 8 * n_rows * n_cols
    feats = 4096

    def along_col(i):
        return (r, lax.rem(c + i, n_cols))

    def along_row(i):
        return (lax.rem(r + i, n_rows), c)

    step = xa.shape[1] // CHUNKS
    loads = []
    for which, (x_hbm, x, w_hbm, w) in enumerate(((act, xa, pin, wa), (outg, xg, pout, wg))):
        for k in range(CHUNKS):
            part = pl.ds(k * step, step)
            pair = (
                pltpu.make_async_copy(w_hbm.at[part, :], w.at[part, :], in_sem.at[2 * which, k]),
                pltpu.make_async_copy(x_hbm.at[:, part], x.at[:, part], in_sem.at[2 * which + 1, k]),
            )
            for cp in pair:
                cp.start()
            loads.append(pair)

    barrier = pltpu.get_barrier_semaphore()

    def greet_col(i, _):
        pl.semaphore_signal(barrier, inc=1, device_id=along_col(i), device_id_type=MESH)
        return 0

    def greet_row(i, _):
        pl.semaphore_signal(barrier, inc=1, device_id=along_row(i), device_id_type=MESH)
        return 0

    lax.fori_loop(1, n_cols, greet_col, 0)
    lax.fori_loop(1, n_rows, greet_row, 0)

    projected = []
    for which, (x, w) in enumerate(((xa, wa), (xg, wg))):
        total = None
        for k in range(CHUNKS):
            for cp in loads[which * CHUNKS + k]:
                cp.wait()
            part = pl.ds(k * step, step)
            term = nn(x[:, part], w[part, :])
            total = term if total is None else total + term
        projected.append(jnp.concatenate([total, total], axis=1))
    a2, g2 = projected
    a_hi = a2.astype(BF16)
    a_lo = (a2 - a_hi.astype(F32)).astype(BF16)
    gt = g2.T[:64]
    sub = lax.broadcasted_iota(jnp.int32, (8, 256), 0)
    tok = lax.broadcasted_iota(jnp.int32, (8, 256), 1)
    mask = jnp.where(tok // 32 == sub, 1.0, 0.0)
    spread = (gt[:, None, :] * mask[None]).reshape(512, 256)
    s_hi = spread.astype(BF16)
    s_lo = (spread - s_hi.astype(F32)).astype(BF16)
    outer = nn(s_hi, a_hi) + (nn(s_hi, a_lo) + nn(s_lo, a_hi))
    outer = (outer * 32 ** (-0.5)).reshape(32, 2, 8, 128)
    lane = lax.broadcasted_iota(jnp.int32, (8, 128), 1)
    grads = jnp.where((lane < 64)[None], outer[:, 0], outer[:, 1]).astype(BF16)
    wide = grads.astype(F32)
    part_sq = jnp.sum(wide * wide, axis=0)
    sq_hi = part_sq.astype(BF16)
    own[0] = sq_hi
    own[1] = (part_sq - sq_hi.astype(F32)).astype(BF16)
    own[2:34] = grads

    mine8 = pl.ds(pl.multiple_of(8 * c, 8), 8)
    pa[:, mine8, :] = own[0:4]
    ca[:, mine8, :] = own[pl.ds(2 + 4 * c, 4)]
    ra[:, r] = own[pl.ds(2 + 2 * r, 2)]

    pl.semaphore_wait(barrier, n_cols + n_rows - 2)

    def copy_pa(i):
        return pltpu.make_async_remote_copy(
            src_ref=own.at[0:4], dst_ref=pa.at[:, mine8, :], send_sem=pa_s.at[i], recv_sem=pa_r.at[i],
            device_id=along_col(i), device_id_type=MESH)

    def copy_ca(i):
        to = lax.rem(c + i, n_cols)
        return pltpu.make_async_remote_copy(
            src_ref=own.at[pl.ds(2 + 4 * to, 4)], dst_ref=ca.at[:, mine8, :], send_sem=ca_s.at[i],
            recv_sem=ca_r.at[i], device_id=along_col(i), device_id_type=MESH)

    def copy_ra(i):
        to = lax.rem(r + i, n_rows)
        return pltpu.make_async_remote_copy(
            src_ref=own.at[pl.ds(2 + 2 * to, 2)], dst_ref=ra.at[:, r], send_sem=ra_s.at[i],
            recv_sem=ra_r.at[i], device_id=along_row(i), device_id_type=MESH)

    mine64 = pl.ds(pl.multiple_of(64 * r, 64), 64)

    def copy_pb(i):
        return pltpu.make_async_remote_copy(
            src_ref=pa.at[2:4], dst_ref=pb.at[:, mine64, :], send_sem=pb_s.at[i], recv_sem=pb_r.at[i],
            device_id=along_row(i), device_id_type=MESH)

    def copy_sq(i):
        return pltpu.make_async_remote_copy(
            src_ref=own_sq, dst_ref=sq.at[r], send_sem=sq_s.at[i], recv_sem=sq_r.at[i],
            device_id=along_row(i), device_id_type=MESH)

    def copy_cb(i):
        return pltpu.make_async_remote_copy(
            src_ref=ca, dst_ref=cb.at[:, mine64, :], send_sem=cb_s.at[i], recv_sem=cb_r.at[i],
            device_id=along_row(i), device_id_type=MESH)

    def copy_rb(i):
        return pltpu.make_async_remote_copy(
            src_ref=ra, dst_ref=rb.at[:, :, mine8, :], send_sem=rb_s.at[i], recv_sem=rb_r.at[i],
            device_id=along_col(i), device_id_type=MESH)

    def each(count, copies, act_on):
        def run(i, _):
            for copy in copies:
                getattr(copy(i), act_on)()
            return 0

        lax.fori_loop(1, count, run, 0)

    each(n_cols, (copy_pa,), "start")
    each(n_cols, (copy_ca,), "start")
    each(n_rows, (copy_ra,), "start")

    each(n_cols, (copy_pa,), "wait_recv")
    sums = (pa[0].astype(F32) + pa[1].astype(F32)).reshape(8, 8, 128)
    part_sq = jnp.sum(sums, axis=0)
    sq_hi = part_sq.astype(BF16)
    own_sq[0] = sq_hi
    own_sq[1] = (part_sq - sq_hi.astype(F32)).astype(BF16)
    sq[r] = own_sq[...]
    pb[:, mine64, :] = pa[2:4]
    each(n_rows, (copy_pb, copy_sq), "start")

    each(n_cols, (copy_ca,), "wait_recv")
    cb[:, mine64, :] = ca[...]
    each(n_rows, (copy_cb,), "start")
    each(n_rows, (copy_ra,), "wait_recv")
    rb[:, :, mine8, :] = ra[...]
    each(n_cols, (copy_rb,), "start")

    each(n_rows, (copy_pb, copy_sq), "wait_recv")
    all_sq = jnp.sum(sq[:, 0].astype(F32) + sq[:, 1].astype(F32), axis=0)
    all_sq = jnp.sum(jnp.sum(all_sq, axis=1, keepdims=True), axis=0, keepdims=True)
    damping = all_sq * (damp_coef / (total_ex * feats))
    gp = jnp.concatenate([pb[0], pb[1]], axis=1)
    gpt = gp.T
    diag_block = nn(gpt, gp)
    i0 = lax.broadcasted_iota(jnp.int32, (256, 256), 0)
    i1 = lax.broadcasted_iota(jnp.int32, (256, 256), 1)
    lev = damp[0:1, 0:256].astype(F32)
    inv_damp = 1.0 / damping
    amat[...] = diag_block * (inv_damp * (1.0 / total_ex)) + jnp.where(i0 == i1, lev, 0.0)

    def emit_to(ref):
        def emit(i, v):
            ref[i : i + 1, :] = v

        return emit

    inv_chol(amat[0:128, 0:128].reshape(16, 8, 128), emit_to(inv1))
    l21 = nt(amat[128:256, 0:128], inv1[...], HIGHEST)
    a22 = amat[128:256, 128:256] - nt(l21, l21, HIGHEST)

    each(n_rows, (copy_cb,), "wait_recv")
    each(n_cols, (copy_rb,), "wait_recv")
    gr = jnp.concatenate([rb[0].reshape(1024, 128), rb[1].reshape(1024, 128)], axis=1)
    gc = jnp.concatenate([cb[q] for q in range(4)], axis=1)
    grt = gr.T
    scale = 1.0 / total_ex
    f_rp = nn(grt, gp) * scale
    f_pc = nn(gpt, gc) * scale
    f_rc = nn(grt, gc) * scale

    inv_chol(a22.reshape(16, 8, 128), emit_to(inv2))
    x1 = nt(f_rp[:, 0:128], inv1[...], HIGHEST)
    y1 = nn(inv1[...], f_pc[0:128], HIGHEST)
    x2 = nt(f_rp[:, 128:256] - nt(x1, l21, HIGHEST), inv2[...], HIGHEST)
    y2 = nn(inv2[...], f_pc[128:256] - nn(l21, y1, HIGHEST), HIGHEST)
    root = lax.rsqrt(damping)
    left = jnp.concatenate([x1, x2], axis=1)
    right = jnp.concatenate([y1, y2], axis=0)
    row_glob = 256 * r + lax.broadcasted_iota(jnp.int32, (256, 512), 0)
    col_glob = 512 * c + lax.broadcasted_iota(jnp.int32, (256, 512), 1)
    levels = damp[pl.ds(c, 1), :].astype(F32)
    out[...] = (f_rc + jnp.where(row_glob == col_glob, damping * levels, 0.0)) - nn(left, right, HIGHEST) * inv_damp

    @pl.when(c == 0)
    def _():
        out[:, 0:256] = left * root

    @pl.when(r == 0)
    def _():
        out[...] = jnp.zeros_like(out)

    @pl.when((r == 0) & (c == 0))
    def _():
        size = damping * root
        tri = i0[0:128, 0:128] >= i1[0:128, 0:128]
        l11 = nt(amat[0:128, 0:128], inv1[...], HIGHEST)
        l22 = nt(a22, inv2[...], HIGHEST)
        out[0:128, 0:128] = jnp.where(tri, l11, 0.0) * size
        out[128:256, 0:128] = l21 * size
        out[128:256, 128:256] = jnp.where(tri, l22, 0.0) * size

    each(n_cols, (copy_pa, copy_ca, copy_rb), "wait_send")
    each(n_rows, (copy_ra, copy_pb, copy_sq, copy_cb), "wait_send")


def shards(n_rows, n_cols, activations, out_grads, proj_in, proj_out, damp_level):
    ex, tok, width = activations.shape
    dma = pltpu.SemaphoreType.DMA
    n, m = dma((n_rows,)), dma((n_cols,))
    any_spec = pl.BlockSpec(memory_space=pl.ANY)
    return pl.pallas_call(
        functools.partial(body, n_rows, n_cols),
        out_shape=jax.ShapeDtypeStruct((256, 512), F32),
        in_specs=[any_spec] * 4 + [pl.BlockSpec(memory_space=pltpu.VMEM)],
        out_specs=pl.BlockSpec(memory_space=pltpu.VMEM),
        scratch_shapes=[
            pltpu.VMEM((ex * tok, width), BF16),
            pltpu.VMEM((ex * tok, width), BF16),
            pltpu.VMEM((width, 64), BF16),
            pltpu.VMEM((width, 64), BF16),
            pltpu.VMEM((34, 8, 128), BF16),
            pltpu.VMEM((4, 64, 128), BF16),
            pltpu.VMEM((4, 64, 128), BF16),
            pltpu.VMEM((2, 16, 8, 128), BF16),
            pltpu.VMEM((2, 8, 128), BF16),
            pltpu.VMEM((2, 1024, 128), BF16),
            pltpu.VMEM((16, 2, 8, 128), BF16),
            pltpu.VMEM((4, 1024, 128), BF16),
            pltpu.VMEM((2, 16, 64, 128), BF16),
            pltpu.VMEM((256, 256), F32),
            pltpu.VMEM((128, 128), F32),
            pltpu.VMEM((128, 128), F32),
            dma((4, CHUNKS)),
            m, m, m, m, n, n, n, n, n, n, n, n, m, m,
        ],
        compiler_params=pltpu.CompilerParams(collective_id=0, has_side_effects=True),
        name="fisher",
    )(
        activations.reshape(ex * tok, width),
        out_grads.reshape(ex * tok, width),
        proj_in,
        proj_out,
        damp_level.reshape(8, 512),
    )


def solution(mesh):
    return jax.shard_map(
        functools.partial(shards, mesh.shape["row"], mesh.shape["col"]),
        mesh=mesh,
        in_specs=(P(("row", "col"), None, None), P(("row", "col"), None, None), P(), P(), P()),
        out_specs=P("row", "col"),
        check_vma=False,
    )
```

```python
import functools

import jax
import jax.numpy as jnp
from jax import lax
from jax.experimental import pallas as pl
from jax.experimental.pallas import tpu as pltpu
from jax.sharding import PartitionSpec as P

F32, BF16 = jnp.float32, jnp.bfloat16
MESH = pl.DeviceIdType.MESH
HIGHEST = lax.Precision.HIGHEST
PANEL = 128
damp_coef = 0.25
CHUNKS = 8


def nn(a, b, precision=None):
    return lax.dot_general(a, b, (((1,), (0,)), ((), ())), precision=precision, preferred_element_type=F32)


def nt(a, b, precision=None):
    return lax.dot_general(a, b, (((1,), (1,)), ((), ())), precision=precision, preferred_element_type=F32)


def inv_chol(m3, emit, midway=None):
    lane = lax.broadcasted_iota(jnp.int32, (8, 128), 1)
    for k in range(16):
        if k == 4 and midway is not None:
            midway()
        for o in (0, 4):
            j = 8 * k + o
            inside = (lane >= j) & (lane < j + 4)
            cols = [jnp.broadcast_to(m3[:, :, j + a : j + a + 1], m3.shape) for a in range(4)]

            def splat(b, a):
                return jnp.broadcast_to(cols[a][0, o + b : o + b + 1, :], (8, 128))

            def row(b):
                wide = jnp.broadcast_to(m3[0, o + b : o + b + 1, :], (8, 128))
                return jnp.where(inside, jnp.where(lane == j + b, 1.0, 0.0), wide)

            p00, p10, p11 = splat(0, 0), splat(1, 0), splat(1, 1)
            q00, q01, q10, q11 = splat(2, 0), splat(2, 1), splat(3, 0), splat(3, 1)
            p22, p32, p33 = splat(2, 2), splat(3, 2), splat(3, 3)
            r0, r1, r2, r3 = (row(b) for b in range(4))
            d1 = 1.0 / (p00 * p11 - p10 * p10)
            i00, i01, i11 = p11 * d1, -p10 * d1, p00 * d1
            t00, t01 = q00 * i00 + q01 * i01, q00 * i01 + q01 * i11
            t10, t11 = q10 * i00 + q11 * i01, q10 * i01 + q11 * i11
            s00 = p22 - (t00 * q00 + t01 * q01)
            s10 = p32 - (t10 * q00 + t11 * q01)
            s11 = p33 - (t10 * q10 + t11 * q11)
            d2 = 1.0 / (s00 * s11 - s10 * s10)
            y2 = r2 - (t00 * r0 + t01 * r1)
            y3 = r3 - (t10 * r0 + t11 * r1)
            e00, e01, e11 = s11 * d2, -s10 * d2, s00 * d2
            w2 = e00 * y2 + e01 * y3
            w3 = e01 * y2 + e11 * y3
            w0 = (i00 * r0 + i01 * r1) - (t00 * w2 + t10 * w3)
            w1 = (i01 * r0 + i11 * r1) - (t01 * w2 + t11 * w3)
            u0 = lax.rsqrt(p00)
            f1 = p10 * (u0 * u0)
            g1 = lax.rsqrt(p11 - f1 * p10)
            u2 = lax.rsqrt(s00)
            f3 = s10 * (u2 * u2)
            g3 = lax.rsqrt(s11 - f3 * s10)
            keep = lane < j + 4
            rows = (r0 * u0, (r1 - f1 * r0) * g1, y2 * u2, (y3 - f3 * y2) * g3)
            for b in range(4):
                emit(j + b, jnp.where(keep, rows[b], 0.0)[0:1, :])
            if j + 4 < PANEL:
                base = jnp.where(inside[None], 0.0, m3)
                m3 = base - (cols[0] * w0[None] + cols[1] * w1[None] + cols[2] * w2[None] + cols[3] * w3[None])
        if k < 15:
            m3 = m3[1:]


def body(
    n_rows, n_cols, act, outg, pin, pout, damp_hbm, out,
    xa, xg, wa, wg, damp, own, own_sq, sq, ca, ra, p0, p1, cb, rb, amat, inv1, inv2,
    in_sem, damp_sem, p0_s, p0_r, p1_s, p1_r, sq_s, sq_r, ca_s, ca_r, ra_s, ra_r, c0_s, c0_r, c1_s, c1_r, rb_s, rb_r,
):
    r, c = lax.axis_index("row"), lax.axis_index("col")
    me = r * n_cols + c
    count = n_rows * n_cols
    total_ex = 8 * count
    feats = 4096
    later_cols = [lax.rem(c + j, n_cols) for j in range(n_cols)]

    def to_all(act_on):
        for j in range(1, n_cols):
            act_on((r, later_cols[j]))

        def run(i, _):
            row = lax.rem(r + i, n_rows)
            for j in range(n_cols):
                act_on((row, later_cols[j]))
            return 0

        lax.fori_loop(1, n_rows, run, 0)

    barrier = pltpu.get_barrier_semaphore()
    to_all(lambda to: pl.semaphore_signal(barrier, inc=1, device_id=to, device_id_type=MESH))

    step = xa.shape[1] // CHUNKS
    loads = []
    for k in range(CHUNKS):
        part = pl.ds(k * step, step)
        copies = []
        for which, (hbm, vmem) in enumerate(((pin, wa), (act, xa), (pout, wg), (outg, xg))):
            copies.append(pltpu.make_async_copy(hbm.at[:, part], vmem.at[:, part], in_sem.at[which, k]))
            copies[-1].start()
        loads.append(copies)
    damp_load = pltpu.make_async_copy(damp_hbm, damp, damp_sem)
    damp_load.start()

    a1 = gt = None
    for k in range(CHUNKS):
        for cp in loads[k]:
            cp.wait()
        part = pl.ds(k * step, step)
        a_term = nt(xa[:, part], wa[:, part])
        g_term = nt(wg[:, part], xg[:, part])
        a1, gt = (a_term, g_term) if k == 0 else (a1 + a_term, gt + g_term)
    a2 = jnp.concatenate([a1, a1], axis=1)
    a_hi = a2.astype(BF16)
    a_lo = (a2 - a_hi.astype(F32)).astype(BF16)
    sub = lax.broadcasted_iota(jnp.int32, (8, 256), 0)
    tok = lax.broadcasted_iota(jnp.int32, (8, 256), 1)
    mask = jnp.where(tok // 32 == sub, 1.0, 0.0)
    spread = (gt[:, None, :] * mask[None]).reshape(512, 256)
    s_hi = spread.astype(BF16)
    s_lo = (spread - s_hi.astype(F32)).astype(BF16)
    outer = nn(s_hi, a_hi) + (nn(s_hi, a_lo) + nn(s_lo, a_hi))
    outer = (outer * 32 ** (-0.5)).reshape(32, 2, 8, 128)
    lane = lax.broadcasted_iota(jnp.int32, (8, 128), 1)
    grads = jnp.where((lane < 64)[None], outer[:, 0], outer[:, 1]).astype(BF16)
    wide = grads.astype(F32)
    part_sq = jnp.sum(jnp.sum(wide * wide, axis=0), axis=0, keepdims=True)
    sq_hi = part_sq.astype(BF16).astype(F32)
    own[...] = grads
    own_sq[...] = jnp.concatenate([sq_hi, part_sq - sq_hi], axis=0).astype(BF16)
    sq[me] = own_sq[...]
    p0[me] = own[0]
    p1[me] = own[1]
    mine8 = pl.ds(pl.multiple_of(8 * c, 8), 8)
    ca[:, mine8, :] = own[pl.ds(4 * c, 4)]
    ra[:, r] = own[pl.ds(2 * r, 2)]

    pl.semaphore_wait(barrier, count - 1)

    def along_col(i):
        return (r, lax.rem(c + i, n_cols))

    def along_row(i):
        return (lax.rem(r + i, n_rows), c)

    def remote(src, dst, send, recv, to):
        return pltpu.make_async_remote_copy(
            src_ref=src, dst_ref=dst, send_sem=send, recv_sem=recv, device_id=to, device_id_type=MESH)

    def copy_p0(to):
        return remote(own.at[0], p0.at[me], p0_s, p0_r, to)

    def copy_p1(to):
        return remote(own.at[1], p1.at[me], p1_s, p1_r, to)

    def copy_sq(to):
        return remote(own_sq, sq.at[me], sq_s, sq_r, to)

    def copy_ca(i):
        to = lax.rem(c + i, n_cols)
        return remote(own.at[pl.ds(4 * to, 4)], ca.at[:, mine8, :], ca_s.at[i], ca_r.at[i], along_col(i))

    def copy_ra(i):
        to = lax.rem(r + i, n_rows)
        return remote(own.at[pl.ds(2 * to, 2)], ra.at[:, r], ra_s.at[i], ra_r.at[i], along_row(i))

    x, y = lax.rem(r, 4), r // 4

    def peer(axis, i):
        return 4 * y + lax.rem(x + i, 4) if axis == 0 else 4 * lax.rem(y + i, 4) + x

    def c_block(half, row):
        return cb.at[2 * half : 2 * half + 2, pl.ds(pl.multiple_of(64 * row, 64), 64), :]

    def copy_c0(half, i):
        return remote(ca.at[2 * half : 2 * half + 2], c_block(half, r), c0_s.at[half, i], c0_r.at[half, i],
                      (peer(half, i), c))

    def copy_c1(half, b, i):
        row = peer(half, 4 - b) if b else r
        src = c_block(half, row) if b else ca.at[2 * half : 2 * half + 2]
        return remote(src, c_block(half, row), c1_s.at[half, b, i], c1_r.at[half, b, i], (peer(1 - half, i), c))

    def copy_rb(i):
        return remote(ra, rb.at[:, :, mine8, :], rb_s.at[i], rb_r.at[i], along_col(i))

    def each(number, copies, act_on):
        def run(i, _):
            for copy in copies:
                getattr(copy(i), act_on)()
            return 0

        lax.fori_loop(1, number, run, 0)

    def all_of(ref, sem):
        others = ref.at[0 : count - 1]
        pltpu.make_async_copy(others, others, sem).wait()

    def send_panel(to):
        copy_p0(to).start()
        copy_sq(to).start()

    to_all(send_panel)
    each(n_cols, (copy_ca,), "start")
    each(n_rows, (copy_ra,), "start")
    to_all(lambda to: copy_p1(to).start())

    each(n_cols, (copy_ca,), "wait_recv")
    for half in range(2):
        for i in (1, 2, 3):
            copy_c0(half, i).start()
    for half in range(2):
        c_block(half, r)[...] = ca[2 * half : 2 * half + 2]
        for i in (1, 2, 3):
            copy_c1(half, 0, i).start()
    each(n_rows, (copy_ra,), "wait_recv")
    rb[:, :, mine8, :] = ra[...]
    each(n_cols, (copy_rb,), "start")

    def forward():
        for b in (1, 2, 3):
            for half in range(2):
                copy_c0(half, b).wait_recv()
                for i in (1, 2, 3):
                    copy_c1(half, b, i).start()

    damp_load.wait()
    scale = 1.0 / total_ex
    i0 = lax.broadcasted_iota(jnp.int32, (128, 128), 0)
    i1 = lax.broadcasted_iota(jnp.int32, (128, 128), 1)
    all_of(p0, p0_r)
    g0 = p0[...].reshape(1024, 128)
    g0t = g0.T
    f00 = nn(g0t, g0)
    all_of(sq, sq_r)
    all_sq = jnp.sum(sq[...].astype(F32), axis=0)
    all_sq = jnp.sum(jnp.sum(all_sq, axis=1, keepdims=True), axis=0, keepdims=True)
    damping = all_sq * (damp_coef / (total_ex * feats))
    inv_damp = 1.0 / damping
    unit = inv_damp * scale
    lev0 = damp[0:128].reshape(1, 128).astype(F32)
    lev1 = damp[128:256].reshape(1, 128).astype(F32)
    amat[0] = f00 * unit + jnp.where(i0 == i1, lev0, 0.0)

    def emit_to(ref):
        def emit(i, v):
            ref[i : i + 1, :] = v

        return emit

    inv_chol(amat[0].reshape(16, 8, 128), emit_to(inv1), forward)

    all_of(p1, p1_r)
    g1 = p1[...].reshape(1024, 128)
    g1t = g1.T
    f10 = nn(g1t, g0)
    f11 = nn(g1t, g1)
    l21 = nt(f10 * unit, inv1[...], HIGHEST)
    a22 = (f11 * unit + jnp.where(i0 == i1, lev1, 0.0)) - nt(l21, l21, HIGHEST)
    amat[1] = a22

    inv_chol(amat[1].reshape(16, 8, 128), emit_to(inv2))
    for half in range(2):
        for b in range(4):
            for i in (1, 2, 3):
                copy_c1(half, b, i).wait_recv()
    each(n_cols, (copy_rb,), "wait_recv")
    gr = jnp.concatenate([rb[0].reshape(1024, 128), rb[1].reshape(1024, 128)], axis=1)
    gc = jnp.concatenate([cb[q] for q in range(4)], axis=1)
    grt = gr.T
    f_rp0 = nn(grt, g0) * scale
    f_rp1 = nn(grt, g1) * scale
    f_pc0 = nn(g0t, gc) * scale
    f_pc1 = nn(g1t, gc) * scale
    f_rc = nn(grt, gc) * scale

    x1 = nt(f_rp0, inv1[...], HIGHEST)
    y1 = nn(inv1[...], f_pc0, HIGHEST)
    x2 = nt(f_rp1 - nt(x1, l21, HIGHEST), inv2[...], HIGHEST)
    y2 = nn(inv2[...], f_pc1 - nn(l21, y1, HIGHEST), HIGHEST)
    root = lax.rsqrt(damping)
    left = jnp.concatenate([x1, x2], axis=1)
    right = jnp.concatenate([y1, y2], axis=0)
    row_glob = 256 * r + lax.broadcasted_iota(jnp.int32, (256, 512), 0)
    col_glob = 512 * c + lax.broadcasted_iota(jnp.int32, (256, 512), 1)
    levels = damp[pl.ds(pl.multiple_of(512 * c, 512), 512)].reshape(1, 512).astype(F32)
    out[...] = (f_rc + jnp.where(row_glob == col_glob, damping * levels, 0.0)) - nn(left, right, HIGHEST) * inv_damp

    @pl.when(c == 0)
    def _():
        out[:, 0:256] = left * root

    @pl.when(r == 0)
    def _():
        out[...] = jnp.zeros_like(out)

    @pl.when((r == 0) & (c == 0))
    def _():
        size = damping * root
        l11 = nt(amat[0], inv1[...], HIGHEST)
        l22 = nt(amat[1], inv2[...], HIGHEST)
        out[0:128, 0:128] = jnp.where(i0 >= i1, l11, 0.0) * size
        out[128:256, 0:128] = l21 * size
        out[128:256, 128:256] = jnp.where(i0 >= i1, l22, 0.0) * size

    each(n_cols, (copy_ca, copy_rb), "wait_send")
    each(n_rows, (copy_ra,), "wait_send")
    for half in range(2):
        for i in (1, 2, 3):
            copy_c0(half, i).wait_send()
            for b in range(4):
                copy_c1(half, b, i).wait_send()
    all_of(p0, p0_s)
    all_of(p1, p1_s)
    all_of(sq, sq_s)


def shards(n_rows, n_cols, activations, out_grads, proj_in, proj_out, damp_level):
    ex, tok, width = activations.shape
    dma = pltpu.SemaphoreType.DMA
    one, n, m = dma(()), dma((n_rows,)), dma((n_cols,))
    return pl.pallas_call(
        functools.partial(body, n_rows, n_cols),
        out_shape=pltpu.VMEM((256, 512), F32),
        in_specs=[pl.BlockSpec(memory_space=pl.ANY)] * 5,
        out_specs=pl.BlockSpec(memory_space=pltpu.VMEM),
        scratch_shapes=[
            pltpu.VMEM((ex * tok, width), BF16),
            pltpu.VMEM((ex * tok, width), BF16),
            pltpu.VMEM((64, width), BF16),
            pltpu.VMEM((64, width), BF16),
            pltpu.VMEM((4096,), jnp.int32),
            pltpu.VMEM((32, 8, 128), BF16),
            pltpu.VMEM((2, 128), BF16),
            pltpu.VMEM((128, 2, 128), BF16),
            pltpu.VMEM((4, 64, 128), BF16),
            pltpu.VMEM((2, 16, 8, 128), BF16),
            pltpu.VMEM((128, 8, 128), BF16),
            pltpu.VMEM((128, 8, 128), BF16),
            pltpu.VMEM((4, 1024, 128), BF16),
            pltpu.VMEM((2, 16, 64, 128), BF16),
            pltpu.VMEM((2, 128, 128), F32),
            pltpu.VMEM((128, 128), F32),
            pltpu.VMEM((128, 128), F32),
            dma((4, CHUNKS)), one,
            one, one, one, one,
            one, one, m, m, n, n, dma((2, 4)), dma((2, 4)), dma((2, 4, 4)), dma((2, 4, 4)), m, m,
        ],
        compiler_params=pltpu.CompilerParams(collective_id=0, has_side_effects=True),
        name="fisher",
    )(
        activations.reshape(ex * tok, width),
        out_grads.reshape(ex * tok, width),
        proj_in.T,
        proj_out.T,
        damp_level,
    )


def solution(mesh):
    return jax.shard_map(
        functools.partial(shards, mesh.shape["row"], mesh.shape["col"]),
        mesh=mesh,
        in_specs=(P(("row", "col"), None, None), P(("row", "col"), None, None), P(), P(), P()),
        out_specs=P("row", "col"),
        check_vma=False,
    )
```

```python
import functools

import jax
import jax.numpy as jnp
from jax import lax
from jax.experimental import pallas as pl
from jax.experimental.pallas import tpu as pltpu
from jax.sharding import PartitionSpec as P

F32, BF16 = jnp.float32, jnp.bfloat16
MESH = pl.DeviceIdType.MESH
HIGHEST = lax.Precision.HIGHEST
PANEL = 128
damp_coef = 0.25
CHUNKS = 8


def nn(a, b, precision=None):
    return lax.dot_general(a, b, (((1,), (0,)), ((), ())), precision=precision, preferred_element_type=F32)


def nt(a, b, precision=None):
    return lax.dot_general(a, b, (((1,), (1,)), ((), ())), precision=precision, preferred_element_type=F32)


def lanes(v, j):
    return jnp.take_along_axis(v, jnp.full(v.shape, j, jnp.int32), axis=1)


def inv_chol(src, dst):
    lane = lax.broadcasted_iota(jnp.int32, (8, 128), 1)
    m = [src[8 * k : 8 * k + 8, :] for k in range(16)]
    for k in range(16):
        for o in (0, 4):
            j = 8 * k + o
            inside = (lane >= j) & (lane < j + 4)
            pivot = [lanes(m[k], j + a) for a in range(4)]

            def splat(b, a):
                return jnp.broadcast_to(pivot[a][o + b : o + b + 1, :], (8, 128))

            def row(b):
                wide = jnp.broadcast_to(m[k][o + b : o + b + 1, :], (8, 128))
                return jnp.where(inside, jnp.where(lane == j + b, 1.0, 0.0), wide)

            p00, p10, p11 = splat(0, 0), splat(1, 0), splat(1, 1)
            q00, q01, q10, q11 = splat(2, 0), splat(2, 1), splat(3, 0), splat(3, 1)
            p22, p32, p33 = splat(2, 2), splat(3, 2), splat(3, 3)
            r0, r1, r2, r3 = (row(b) for b in range(4))
            d1 = 1.0 / (p00 * p11 - p10 * p10)
            i00, i01, i11 = p11 * d1, -p10 * d1, p00 * d1
            t00, t01 = q00 * i00 + q01 * i01, q00 * i01 + q01 * i11
            t10, t11 = q10 * i00 + q11 * i01, q10 * i01 + q11 * i11
            s00 = p22 - (t00 * q00 + t01 * q01)
            s10 = p32 - (t10 * q00 + t11 * q01)
            s11 = p33 - (t10 * q10 + t11 * q11)
            d2 = 1.0 / (s00 * s11 - s10 * s10)
            y2 = r2 - (t00 * r0 + t01 * r1)
            y3 = r3 - (t10 * r0 + t11 * r1)
            e00, e01, e11 = s11 * d2, -s10 * d2, s00 * d2
            w2 = e00 * y2 + e01 * y3
            w3 = e01 * y2 + e11 * y3
            w0 = (i00 * r0 + i01 * r1) - (t00 * w2 + t10 * w3)
            w1 = (i01 * r0 + i11 * r1) - (t01 * w2 + t11 * w3)
            u0 = lax.rsqrt(p00)
            f1 = p10 * (u0 * u0)
            g1 = lax.rsqrt(p11 - f1 * p10)
            u2 = lax.rsqrt(s00)
            f3 = s10 * (u2 * u2)
            g3 = lax.rsqrt(s11 - f3 * s10)
            keep = lane < j + 4
            rows = (r0 * u0, (r1 - f1 * r0) * g1, y2 * u2, (y3 - f3 * y2) * g3)
            for b in range(4):
                dst[j + b : j + b + 1, :] = jnp.where(keep, rows[b], 0.0)[0:1, :]
            for n in range(k if o == 0 else k + 1, 16):
                cols = pivot if n == k else [lanes(m[n], j + a) for a in range(4)]
                m[n] = jnp.where(inside, 0.0, m[n]) - (
                    (cols[0] * w0 + cols[1] * w1) + (cols[2] * w2 + cols[3] * w3)
                )


def body(
    n_rows, n_cols, act, outg, pin, pout, damp_hbm, out,
    xa, xg, wa, wg, damp, own, own_sq, sqa, sqb, sq, ra, p0, p1, cb, rb, amat, inv1, inv2,
    in_sem, damp_sem, p0_s, p0_r, p1_s, p1_r, sqa_s, sqa_r, sq_s, sq_r, ra_s, ra_r, c0_s, c0_r, c1_s, c1_r, rb_s, rb_r,
):
    r, c = lax.axis_index("row"), lax.axis_index("col")
    me = r * n_cols + c
    count = n_rows * n_cols
    total_ex = 8 * count
    feats = 4096
    later_cols = [lax.rem(c + j, n_cols) for j in range(n_cols)]

    def to_all(act_on):
        for j in range(1, n_cols):
            act_on((r, later_cols[j]))

        def run(i, _):
            row = lax.rem(r + i, n_rows)
            for j in range(n_cols):
                act_on((row, later_cols[j]))
            return 0

        lax.fori_loop(1, n_rows, run, 0)

    barrier = pltpu.get_barrier_semaphore()
    to_all(lambda to: pl.semaphore_signal(barrier, inc=1, device_id=to, device_id_type=MESH))

    step = xa.shape[1] // CHUNKS
    loads = []
    for k in range(CHUNKS):
        part = pl.ds(k * step, step)
        copies = []
        for which, (hbm, vmem) in enumerate(((pin, wa), (act, xa), (pout, wg), (outg, xg))):
            copies.append(pltpu.make_async_copy(hbm.at[:, part], vmem.at[:, part], in_sem.at[which, k]))
            copies[-1].start()
        loads.append(copies)
    damp_load = pltpu.make_async_copy(damp_hbm, damp, damp_sem)
    damp_load.start()

    a1 = gt = None
    for k in range(CHUNKS):
        for cp in loads[k]:
            cp.wait()
        part = pl.ds(k * step, step)
        a_term = nt(xa[:, part], wa[:, part])
        g_term = nt(wg[:, part], xg[:, part])
        a1, gt = (a_term, g_term) if k == 0 else (a1 + a_term, gt + g_term)
    a2 = jnp.concatenate([a1, a1], axis=1)
    a_hi = a2.astype(BF16)
    a_lo = (a2 - a_hi.astype(F32)).astype(BF16)
    sub = lax.broadcasted_iota(jnp.int32, (8, 256), 0)
    tok = lax.broadcasted_iota(jnp.int32, (8, 256), 1)
    mask = jnp.where(tok // 32 == sub, 1.0, 0.0)
    spread = (gt[:, None, :] * mask[None]).reshape(512, 256)
    s_hi = spread.astype(BF16)
    s_lo = (spread - s_hi.astype(F32)).astype(BF16)
    outer = nn(s_hi, a_hi) + (nn(s_hi, a_lo) + nn(s_lo, a_hi))
    outer = (outer * 32 ** (-0.5)).reshape(32, 2, 8, 128)
    lane = lax.broadcasted_iota(jnp.int32, (8, 128), 1)
    grads = jnp.where((lane < 64)[None], outer[:, 0], outer[:, 1]).astype(BF16)
    wide = grads.astype(F32)

    def hi_lo(v):
        hi = v.astype(BF16).astype(F32)
        return jnp.concatenate([hi, v - hi], axis=0).astype(BF16)

    own[...] = grads
    own_sq[...] = hi_lo(jnp.sum(jnp.sum(wide * wide, axis=0), axis=0, keepdims=True))
    sqa[c] = own_sq[...]
    p0[me] = own[0]
    mine8 = pl.ds(pl.multiple_of(8 * c, 8), 8)
    x, y = lax.rem(r, 4), r // 4
    p1[me] = own[1]
    cb[:, y, x, mine8, :] = own[pl.ds(4 * c, 4)]
    ra[:, r] = own[pl.ds(2 * r, 2)]

    pl.semaphore_wait(barrier, count - 1)

    def along_col(i):
        return (r, lax.rem(c + i, n_cols))

    def along_row(i):
        return (lax.rem(r + i, n_rows), c)

    def remote(src, dst, send, recv, to):
        return pltpu.make_async_remote_copy(
            src_ref=src, dst_ref=dst, send_sem=send, recv_sem=recv, device_id=to, device_id_type=MESH)

    def copy_p0(to):
        return remote(own.at[0], p0.at[me], p0_s, p0_r, to)

    def copy_p1(to):
        return remote(own.at[1], p1.at[me], p1_s, p1_r, to)

    def copy_sqa(i):
        return remote(own_sq, sqa.at[c], sqa_s.at[i], sqa_r.at[i], along_col(i))

    def copy_sq(i):
        return remote(sqb, sq.at[r], sq_s.at[i], sq_r.at[i], along_row(i))

    def copy_ra(i):
        to = lax.rem(r + i, n_rows)
        return remote(own.at[pl.ds(2 * to, 2)], ra.at[:, r], ra_s.at[i], ra_r.at[i], along_row(i))

    def peer(axis, i):
        return 4 * y + lax.rem(x + i, 4) if axis == 0 else 4 * lax.rem(y + i, 4) + x

    def along_line(half, act_on):
        for i in range(4):
            for j in range(n_cols):
                if i or j:
                    act_on((peer(half, i), later_cols[j]))

    def copy_c0(half, to):
        return remote(own.at[pl.ds(4 * to[1] + 2 * half, 2)], cb.at[2 * half : 2 * half + 2, y, x, mine8, :],
                      c0_s.at[half], c0_r.at[half], to)

    def copy_c1(half, i):
        block = cb.at[0:2, y] if half == 0 else cb.at[2:4, :, x]
        return remote(block, block, c1_s.at[half, i], c1_r.at[half, i], (peer(1 - half, i), c))

    def wait_line(sem):
        others = xa.at[0:8, 0 : 256 * (4 * n_cols - 1)]
        pltpu.make_async_copy(others, others, sem).wait()

    def copy_rb(i):
        return remote(ra, rb.at[c], rb_s.at[i], rb_r.at[i], along_col(i))

    def each(number, copies, act_on):
        def run(i, _):
            for copy in copies:
                getattr(copy(i), act_on)()
            return 0

        lax.fori_loop(1, number, run, 0)

    def all_of(ref, sem):
        others = ref.at[0 : count - 1]
        pltpu.make_async_copy(others, others, sem).wait()

    each(n_cols, (copy_sqa,), "start")
    to_all(lambda to: copy_p0(to).start())
    for half in range(2):
        along_line(half, lambda to: copy_c0(half, to).start())
    each(n_cols, (copy_sqa,), "wait_recv")
    sqb[...] = hi_lo(jnp.sum(jnp.sum(sqa[...].astype(F32), axis=0), axis=0, keepdims=True))
    sq[r] = sqb[...]
    each(n_rows, (copy_sq,), "start")
    each(n_rows, (copy_ra,), "start")
    to_all(lambda to: copy_p1(to).start())

    each(n_rows, (copy_ra,), "wait_recv")
    rb[c] = ra[...]
    each(n_cols, (copy_rb,), "start")
    for half in range(2):
        wait_line(c0_r.at[half])
        for i in (1, 2, 3):
            copy_c1(half, i).start()

    damp_load.wait()
    scale = 1.0 / total_ex
    i0 = lax.broadcasted_iota(jnp.int32, (128, 128), 0)
    i1 = lax.broadcasted_iota(jnp.int32, (128, 128), 1)
    all_of(p0, p0_r)
    g0 = p0[...].reshape(1024, 128)
    g0t = g0.T
    f00 = nn(g0t, g0)
    each(n_rows, (copy_sq,), "wait_recv")
    all_sq = jnp.sum(sq[...].astype(F32), axis=0)
    all_sq = jnp.sum(jnp.sum(all_sq, axis=1, keepdims=True), axis=0, keepdims=True)
    damping = all_sq * (damp_coef / (total_ex * feats))
    inv_damp = 1.0 / damping
    unit = inv_damp * scale
    lev0 = damp[0:128].reshape(1, 128).astype(F32)
    lev1 = damp[128:256].reshape(1, 128).astype(F32)
    amat[0] = f00 * unit + jnp.where(i0 == i1, lev0, 0.0)

    inv_chol(amat.at[0], inv1)

    all_of(p1, p1_r)
    g1 = p1[...].reshape(1024, 128)
    g1t = g1.T
    f10 = nn(g1t, g0)
    f11 = nn(g1t, g1)
    l21 = nt(f10 * unit, inv1[...], HIGHEST)
    a22 = (f11 * unit + jnp.where(i0 == i1, lev1, 0.0)) - nt(l21, l21, HIGHEST)
    amat[1] = a22

    inv_chol(amat.at[1], inv2)
    for half in range(2):
        for i in (1, 2, 3):
            copy_c1(half, i).wait_recv()
    each(n_cols, (copy_rb,), "wait_recv")
    halves = [jnp.swapaxes(rb[:, q].astype(F32), 0, 1).reshape(1024, 128) for q in range(2)]
    gr = jnp.concatenate(halves, axis=1).astype(BF16)
    gc = jnp.concatenate([cb[q].reshape(1024, 128) for q in range(4)], axis=1)
    grt = gr.T
    f_rp0 = nn(grt, g0) * scale
    f_rp1 = nn(grt, g1) * scale
    f_pc0 = nn(g0t, gc) * scale
    f_pc1 = nn(g1t, gc) * scale
    f_rc = nn(grt, gc) * scale

    x1 = nt(f_rp0, inv1[...], HIGHEST)
    y1 = nn(inv1[...], f_pc0, HIGHEST)
    x2 = nt(f_rp1 - nt(x1, l21, HIGHEST), inv2[...], HIGHEST)
    y2 = nn(inv2[...], f_pc1 - nn(l21, y1, HIGHEST), HIGHEST)
    root = lax.rsqrt(damping)
    left = jnp.concatenate([x1, x2], axis=1)
    right = jnp.concatenate([y1, y2], axis=0)
    row_glob = 256 * r + lax.broadcasted_iota(jnp.int32, (256, 512), 0)
    col_glob = 512 * c + lax.broadcasted_iota(jnp.int32, (256, 512), 1)
    levels = damp[pl.ds(pl.multiple_of(512 * c, 512), 512)].reshape(1, 512).astype(F32)
    out[...] = (f_rc + jnp.where(row_glob == col_glob, damping * levels, 0.0)) - nn(left, right, HIGHEST) * inv_damp

    @pl.when(c == 0)
    def _():
        out[:, 0:256] = left * root

    @pl.when(r == 0)
    def _():
        out[...] = jnp.zeros_like(out)

    @pl.when((r == 0) & (c == 0))
    def _():
        size = damping * root
        l11 = nt(amat[0], inv1[...], HIGHEST)
        l22 = nt(amat[1], inv2[...], HIGHEST)
        out[0:128, 0:128] = jnp.where(i0 >= i1, l11, 0.0) * size
        out[128:256, 0:128] = l21 * size
        out[128:256, 128:256] = jnp.where(i0 >= i1, l22, 0.0) * size

    each(n_cols, (copy_sqa, copy_rb), "wait_send")
    each(n_rows, (copy_sq, copy_ra), "wait_send")
    for half in range(2):
        wait_line(c0_s.at[half])
        for i in (1, 2, 3):
            copy_c1(half, i).wait_send()
    all_of(p0, p0_s)
    all_of(p1, p1_s)


def shards(n_rows, n_cols, activations, out_grads, proj_in, proj_out, damp_level):
    ex, tok, width = activations.shape
    dma = pltpu.SemaphoreType.DMA
    one, n, m = dma(()), dma((n_rows,)), dma((n_cols,))
    return pl.pallas_call(
        functools.partial(body, n_rows, n_cols),
        out_shape=pltpu.VMEM((256, 512), F32),
        in_specs=[pl.BlockSpec(memory_space=pl.ANY)] * 5,
        out_specs=pl.BlockSpec(memory_space=pltpu.VMEM),
        scratch_shapes=[
            pltpu.VMEM((ex * tok, width), BF16),
            pltpu.VMEM((ex * tok, width), BF16),
            pltpu.VMEM((64, width), BF16),
            pltpu.VMEM((64, width), BF16),
            pltpu.VMEM((4096,), jnp.int32),
            pltpu.VMEM((32, 8, 128), BF16),
            pltpu.VMEM((2, 128), BF16),
            pltpu.VMEM((8, 2, 128), BF16),
            pltpu.VMEM((2, 128), BF16),
            pltpu.VMEM((16, 2, 128), BF16),
            pltpu.VMEM((2, 16, 8, 128), BF16),
            pltpu.VMEM((128, 8, 128), BF16),
            pltpu.VMEM((128, 8, 128), BF16),
            pltpu.VMEM((4, 4, 4, 64, 128), BF16),
            pltpu.VMEM((8, 2, 16, 8, 128), BF16),
            pltpu.VMEM((2, 128, 128), F32),
            pltpu.VMEM((128, 128), F32),
            pltpu.VMEM((128, 128), F32),
            dma((4, CHUNKS)), one,
            one, one, one, one,
            m, m, n, n, n, n, dma((2,)), dma((2,)), dma((2, 4)), dma((2, 4)), m, m,
        ],
        compiler_params=pltpu.CompilerParams(collective_id=0, has_side_effects=True),
        name="fisher",
    )(
        activations.reshape(ex * tok, width),
        out_grads.reshape(ex * tok, width),
        proj_in.T,
        proj_out.T,
        damp_level,
    )


def solution(mesh):
    return jax.shard_map(
        functools.partial(shards, mesh.shape["row"], mesh.shape["col"]),
        mesh=mesh,
        in_specs=(P(("row", "col"), None, None), P(("row", "col"), None, None), P(), P(), P()),
        out_specs=P("row", "col"),
        check_vma=False,
    )
```

```python
import functools

import jax
import jax.numpy as jnp
from jax import lax
from jax.experimental import pallas as pl
from jax.experimental.pallas import tpu as pltpu
from jax.sharding import PartitionSpec as P

F32, BF16 = jnp.float32, jnp.bfloat16
MESH = pl.DeviceIdType.MESH
HIGHEST = lax.Precision.HIGHEST
PANEL = 128
damp_coef = 0.25
CHUNKS = 8


def nn(a, b, precision=None):
    return lax.dot_general(a, b, (((1,), (0,)), ((), ())), precision=precision, preferred_element_type=F32)


def nt(a, b, precision=None):
    return lax.dot_general(a, b, (((1,), (1,)), ((), ())), precision=precision, preferred_element_type=F32)


def hi_and_lo(v):
    hi = v.astype(BF16)
    return hi, (v - hi.astype(F32)).astype(BF16)


def three(dot, a, b):
    return dot(a[0], b[0]) + (dot(a[0], b[1]) + dot(a[1], b[0]))


def lanes(v, j):
    return jnp.take_along_axis(v, jnp.full(v.shape, j, jnp.int32), axis=1)


def inv_chol(src, dst):
    lane = lax.broadcasted_iota(jnp.int32, (8, 128), 1)
    m = [src[8 * k : 8 * k + 8, :] for k in range(16)]
    for k in range(16):
        for o in (0, 4):
            j = 8 * k + o
            inside = (lane >= j) & (lane < j + 4)
            pivot = [lanes(m[k], j + a) for a in range(4)]

            def splat(b, a):
                return jnp.broadcast_to(pivot[a][o + b : o + b + 1, :], (8, 128))

            def row(b):
                wide = jnp.broadcast_to(m[k][o + b : o + b + 1, :], (8, 128))
                return jnp.where(inside, jnp.where(lane == j + b, 1.0, 0.0), wide)

            p00, p10, p11 = splat(0, 0), splat(1, 0), splat(1, 1)
            q00, q01, q10, q11 = splat(2, 0), splat(2, 1), splat(3, 0), splat(3, 1)
            p22, p32, p33 = splat(2, 2), splat(3, 2), splat(3, 3)
            r0, r1, r2, r3 = (row(b) for b in range(4))
            d1 = 1.0 / (p00 * p11 - p10 * p10)
            i00, i01, i11 = p11 * d1, -p10 * d1, p00 * d1
            t00, t01 = q00 * i00 + q01 * i01, q00 * i01 + q01 * i11
            t10, t11 = q10 * i00 + q11 * i01, q10 * i01 + q11 * i11
            s00 = p22 - (t00 * q00 + t01 * q01)
            s10 = p32 - (t10 * q00 + t11 * q01)
            s11 = p33 - (t10 * q10 + t11 * q11)
            d2 = 1.0 / (s00 * s11 - s10 * s10)
            y2 = r2 - (t00 * r0 + t01 * r1)
            y3 = r3 - (t10 * r0 + t11 * r1)
            e00, e01, e11 = s11 * d2, -s10 * d2, s00 * d2
            w2 = e00 * y2 + e01 * y3
            w3 = e01 * y2 + e11 * y3
            w0 = (i00 * r0 + i01 * r1) - (t00 * w2 + t10 * w3)
            w1 = (i01 * r0 + i11 * r1) - (t01 * w2 + t11 * w3)
            u0 = lax.rsqrt(p00)
            f1 = p10 * (u0 * u0)
            g1 = lax.rsqrt(p11 - f1 * p10)
            u2 = lax.rsqrt(s00)
            f3 = s10 * (u2 * u2)
            g3 = lax.rsqrt(s11 - f3 * s10)
            keep = lane < j + 4
            rows = (r0 * u0, (r1 - f1 * r0) * g1, y2 * u2, (y3 - f3 * y2) * g3)
            for b in range(4):
                dst[j + b : j + b + 1, :] = jnp.where(keep, rows[b], 0.0)[0:1, :]
            for n in range(k if o == 0 else k + 1, 16):
                cols = pivot if n == k else [lanes(m[n], j + a) for a in range(4)]
                m[n] = jnp.where(inside, 0.0, m[n]) - (
                    (cols[0] * w0 + cols[1] * w1) + (cols[2] * w2 + cols[3] * w3)
                )


def body(
    n_rows, n_cols, act, outg, pin, pout, damp_hbm, out,
    xa, xg, wa, wg, damp, own, own_sq, sqa, sqb, sq, ra, p0, p1, cb, rb, amat, inv1, inv2,
    in_sem, damp_sem, p0_s, p0_r, p1_s, p1_r, sqa_s, sqa_r, sq_s, sq_r, ra_s, ra_r, c0_s, c0_r, c1_s, c1_r, rb_s, rb_r,
):
    r, c = lax.axis_index("row"), lax.axis_index("col")
    me = r * n_cols + c
    count = n_rows * n_cols
    total_ex = 8 * count
    feats = 4096
    later_cols = [lax.rem(c + j, n_cols) for j in range(n_cols)]

    def to_all(act_on):
        for j in range(1, n_cols):
            act_on((r, later_cols[j]))

        def run(i, _):
            row = lax.rem(r + i, n_rows)
            for j in range(n_cols):
                act_on((row, later_cols[j]))
            return 0

        lax.fori_loop(1, n_rows, run, 0)

    barrier = pltpu.get_barrier_semaphore()
    to_all(lambda to: pl.semaphore_signal(barrier, inc=1, device_id=to, device_id_type=MESH))

    step = xa.shape[1] // CHUNKS
    loads = []
    for k in range(CHUNKS):
        part = pl.ds(k * step, step)
        copies = []
        for which, (hbm, vmem) in enumerate(((pin, wa), (act, xa), (pout, wg), (outg, xg))):
            copies.append(pltpu.make_async_copy(hbm.at[:, part], vmem.at[:, part], in_sem.at[which, k]))
            copies[-1].start()
        loads.append(copies)
    damp_load = pltpu.make_async_copy(damp_hbm, damp, damp_sem)
    damp_load.start()

    a1 = gt = None
    for k in range(CHUNKS):
        for cp in loads[k]:
            cp.wait()
        part = pl.ds(k * step, step)
        a_term = nt(xa[:, part], wa[:, part])
        g_term = nt(wg[:, part], xg[:, part])
        a1, gt = (a_term, g_term) if k == 0 else (a1 + a_term, gt + g_term)
    a2 = jnp.concatenate([a1, a1], axis=1)
    a_hi = a2.astype(BF16)
    a_lo = (a2 - a_hi.astype(F32)).astype(BF16)
    sub = lax.broadcasted_iota(jnp.int32, (8, 256), 0)
    tok = lax.broadcasted_iota(jnp.int32, (8, 256), 1)
    mask = jnp.where(tok // 32 == sub, 1.0, 0.0)
    spread = (gt[:, None, :] * mask[None]).reshape(512, 256)
    s_hi = spread.astype(BF16)
    s_lo = (spread - s_hi.astype(F32)).astype(BF16)
    outer = nn(s_hi, a_hi) + (nn(s_hi, a_lo) + nn(s_lo, a_hi))
    outer = (outer * 32 ** (-0.5)).reshape(32, 2, 8, 128)
    lane = lax.broadcasted_iota(jnp.int32, (8, 128), 1)
    grads = jnp.where((lane < 64)[None], outer[:, 0], outer[:, 1]).astype(BF16)
    wide = grads.astype(F32)

    def hi_lo(v):
        hi = v.astype(BF16).astype(F32)
        return jnp.concatenate([hi, v - hi], axis=0).astype(BF16)

    own[...] = grads
    own_sq[...] = hi_lo(jnp.sum(jnp.sum(wide * wide, axis=0), axis=0, keepdims=True))
    sqa[c] = own_sq[...]
    p0[me] = own[0]
    mine8 = pl.ds(pl.multiple_of(8 * c, 8), 8)
    x, y = lax.rem(r, 4), r // 4
    p1[me] = own[1]
    cb[:, y, x, mine8, :] = own[pl.ds(4 * c, 4)]
    ra[:, r] = own[pl.ds(2 * r, 2)]

    pl.semaphore_wait(barrier, count - 1)

    def along_col(i):
        return (r, lax.rem(c + i, n_cols))

    def along_row(i):
        return (lax.rem(r + i, n_rows), c)

    def remote(src, dst, send, recv, to):
        return pltpu.make_async_remote_copy(
            src_ref=src, dst_ref=dst, send_sem=send, recv_sem=recv, device_id=to, device_id_type=MESH)

    def copy_p0(to):
        return remote(own.at[0], p0.at[me], p0_s, p0_r, to)

    def copy_p1(to):
        return remote(own.at[1], p1.at[me], p1_s, p1_r, to)

    def copy_sqa(i):
        return remote(own_sq, sqa.at[c], sqa_s.at[i], sqa_r.at[i], along_col(i))

    def copy_sq(i):
        return remote(sqb, sq.at[r], sq_s.at[i], sq_r.at[i], along_row(i))

    def copy_ra(i):
        to = lax.rem(r + i, n_rows)
        return remote(own.at[pl.ds(2 * to, 2)], ra.at[:, r], ra_s.at[i], ra_r.at[i], along_row(i))

    def peer(axis, i):
        return 4 * y + lax.rem(x + i, 4) if axis == 0 else 4 * lax.rem(y + i, 4) + x

    def along_line(half, act_on):
        for i in range(4):
            for j in range(n_cols):
                if i or j:
                    act_on((peer(half, i), later_cols[j]))

    def copy_c0(half, to):
        return remote(own.at[pl.ds(4 * to[1] + 2 * half, 2)], cb.at[2 * half : 2 * half + 2, y, x, mine8, :],
                      c0_s.at[half], c0_r.at[half], to)

    def copy_c1(half, i):
        block = cb.at[0:2, y] if half == 0 else cb.at[2:4, :, x]
        return remote(block, block, c1_s.at[half, i], c1_r.at[half, i], (peer(1 - half, i), c))

    def wait_line(sem):
        others = xa.at[0:8, 0 : 256 * (4 * n_cols - 1)]
        pltpu.make_async_copy(others, others, sem).wait()

    def copy_rb(i):
        return remote(ra, rb.at[c], rb_s.at[i], rb_r.at[i], along_col(i))

    def each(number, copies, act_on):
        def run(i, _):
            for copy in copies:
                getattr(copy(i), act_on)()
            return 0

        lax.fori_loop(1, number, run, 0)

    def all_of(ref, sem):
        others = ref.at[0 : count - 1]
        pltpu.make_async_copy(others, others, sem).wait()

    each(n_cols, (copy_sqa,), "start")
    to_all(lambda to: copy_p0(to).start())
    for half in range(2):
        along_line(half, lambda to: copy_c0(half, to).start())
    each(n_cols, (copy_sqa,), "wait_recv")
    sqb[...] = hi_lo(jnp.sum(jnp.sum(sqa[...].astype(F32), axis=0), axis=0, keepdims=True))
    sq[r] = sqb[...]
    each(n_rows, (copy_sq,), "start")
    each(n_rows, (copy_ra,), "start")
    to_all(lambda to: copy_p1(to).start())

    each(n_rows, (copy_ra,), "wait_recv")
    rb[c] = ra[...]
    each(n_cols, (copy_rb,), "start")
    for half in range(2):
        wait_line(c0_r.at[half])
        for i in (1, 2, 3):
            copy_c1(half, i).start()

    damp_load.wait()
    scale = 1.0 / total_ex
    i0 = lax.broadcasted_iota(jnp.int32, (128, 128), 0)
    i1 = lax.broadcasted_iota(jnp.int32, (128, 128), 1)
    all_of(p0, p0_r)
    g0 = p0[...].reshape(1024, 128)
    g0t = g0.T
    f00 = nn(g0t, g0)
    each(n_rows, (copy_sq,), "wait_recv")
    all_sq = jnp.sum(sq[...].astype(F32), axis=0)
    all_sq = jnp.sum(jnp.sum(all_sq, axis=1, keepdims=True), axis=0, keepdims=True)
    damping = all_sq * (damp_coef / (total_ex * feats))
    inv_damp = 1.0 / damping
    unit = inv_damp * scale
    lev0 = damp[0:128].reshape(1, 128).astype(F32)
    lev1 = damp[128:256].reshape(1, 128).astype(F32)
    amat[0] = f00 * unit + jnp.where(i0 == i1, lev0, 0.0)

    inv_chol(amat.at[0], inv1)

    all_of(p1, p1_r)
    g1 = p1[...].reshape(1024, 128)
    g1t = g1.T
    f10 = nn(g1t, g0)
    f11 = nn(g1t, g1)
    l21 = nt(f10 * unit, inv1[...], HIGHEST)
    a22 = (f11 * unit + jnp.where(i0 == i1, lev1, 0.0)) - nt(l21, l21, HIGHEST)
    amat[1] = a22

    inv_chol(amat.at[1], inv2)
    for half in range(2):
        for i in (1, 2, 3):
            copy_c1(half, i).wait_recv()
    each(n_cols, (copy_rb,), "wait_recv")
    halves = [jnp.swapaxes(rb[:, q].astype(F32), 0, 1).reshape(1024, 128) for q in range(2)]
    gr = jnp.concatenate(halves, axis=1).astype(BF16)
    gc = jnp.concatenate([cb[q].reshape(1024, 128) for q in range(4)], axis=1)
    grt = gr.T
    f_rp0 = nn(grt, g0) * scale
    f_rp1 = nn(grt, g1) * scale
    f_pc0 = nn(g0t, gc) * scale
    f_pc1 = nn(g1t, gc) * scale
    f_rc = nn(grt, gc) * scale

    low, first_inv, second_inv = hi_and_lo(l21), hi_and_lo(inv1[...]), hi_and_lo(inv2[...])
    x1 = three(nt, hi_and_lo(f_rp0), first_inv)
    y1 = three(nn, first_inv, hi_and_lo(f_pc0))
    x2 = three(nt, hi_and_lo(f_rp1 - three(nt, hi_and_lo(x1), low)), second_inv)
    y2 = three(nn, second_inv, hi_and_lo(f_pc1 - three(nn, low, hi_and_lo(y1))))
    root = lax.rsqrt(damping)
    left = jnp.concatenate([x1, x2], axis=1)
    right = jnp.concatenate([y1, y2], axis=0)
    row_glob = 256 * r + lax.broadcasted_iota(jnp.int32, (256, 512), 0)
    col_glob = 512 * c + lax.broadcasted_iota(jnp.int32, (256, 512), 1)
    levels = damp[pl.ds(pl.multiple_of(512 * c, 512), 512)].reshape(1, 512).astype(F32)
    out[...] = (f_rc + jnp.where(row_glob == col_glob, damping * levels, 0.0)) - three(nn, hi_and_lo(left), hi_and_lo(right)) * inv_damp

    @pl.when(c == 0)
    def _():
        out[:, 0:256] = left * root

    @pl.when(r == 0)
    def _():
        out[...] = jnp.zeros_like(out)

    @pl.when((r == 0) & (c == 0))
    def _():
        size = damping * root
        l11 = nt(amat[0], inv1[...], HIGHEST)
        l22 = nt(amat[1], inv2[...], HIGHEST)
        out[0:128, 0:128] = jnp.where(i0 >= i1, l11, 0.0) * size
        out[128:256, 0:128] = l21 * size
        out[128:256, 128:256] = jnp.where(i0 >= i1, l22, 0.0) * size

    each(n_cols, (copy_sqa, copy_rb), "wait_send")
    each(n_rows, (copy_sq, copy_ra), "wait_send")
    for half in range(2):
        wait_line(c0_s.at[half])
        for i in (1, 2, 3):
            copy_c1(half, i).wait_send()
    all_of(p0, p0_s)
    all_of(p1, p1_s)


def shards(n_rows, n_cols, activations, out_grads, proj_in, proj_out, damp_level):
    ex, tok, width = activations.shape
    dma = pltpu.SemaphoreType.DMA
    one, n, m = dma(()), dma((n_rows,)), dma((n_cols,))
    return pl.pallas_call(
        functools.partial(body, n_rows, n_cols),
        out_shape=pltpu.VMEM((256, 512), F32),
        in_specs=[pl.BlockSpec(memory_space=pl.ANY)] * 5,
        out_specs=pl.BlockSpec(memory_space=pltpu.VMEM),
        scratch_shapes=[
            pltpu.VMEM((ex * tok, width), BF16),
            pltpu.VMEM((ex * tok, width), BF16),
            pltpu.VMEM((64, width), BF16),
            pltpu.VMEM((64, width), BF16),
            pltpu.VMEM((4096,), jnp.int32),
            pltpu.VMEM((32, 8, 128), BF16),
            pltpu.VMEM((2, 128), BF16),
            pltpu.VMEM((8, 2, 128), BF16),
            pltpu.VMEM((2, 128), BF16),
            pltpu.VMEM((16, 2, 128), BF16),
            pltpu.VMEM((2, 16, 8, 128), BF16),
            pltpu.VMEM((128, 8, 128), BF16),
            pltpu.VMEM((128, 8, 128), BF16),
            pltpu.VMEM((4, 4, 4, 64, 128), BF16),
            pltpu.VMEM((8, 2, 16, 8, 128), BF16),
            pltpu.VMEM((2, 128, 128), F32),
            pltpu.VMEM((128, 128), F32),
            pltpu.VMEM((128, 128), F32),
            dma((4, CHUNKS)), one,
            one, one, one, one,
            m, m, n, n, n, n, dma((2,)), dma((2,)), dma((2, 4)), dma((2, 4)), m, m,
        ],
        compiler_params=pltpu.CompilerParams(collective_id=0, has_side_effects=True),
        name="fisher",
    )(
        activations.reshape(ex * tok, width),
        out_grads.reshape(ex * tok, width),
        proj_in.T,
        proj_out.T,
        damp_level,
    )


def solution(mesh):
    return jax.shard_map(
        functools.partial(shards, mesh.shape["row"], mesh.shape["col"]),
        mesh=mesh,
        in_specs=(P(("row", "col"), None, None), P(("row", "col"), None, None), P(), P(), P()),
        out_specs=P("row", "col"),
        check_vma=False,
    )
```
